32 devices in a mesh: ba: 4 (over z), aa: 8 (over y, x, core).
Axes of the slice: x: 2, y: 2, z: 4, core: 2. Of those that a mesh axis runs over, the one named last changes fastest.
Arguments:
- tokens: bfloat16 [6144, 1024], P(('ba', 'aa')), parts along dimension 0, may hold values from -6 to 6
- latents: bfloat16 [1024, 1024], P(('ba', 'aa')), parts along dimension 0, may hold values from -6 to 6
- read_query: bfloat16 [1024, 512], replicated, may hold values from -0.1875 to 0.1875
- read_keyval: bfloat16 [1024, 1024], replicated, may hold values from -0.1875 to 0.1875
- read_out: bfloat16 [512, 1024], replicated, may hold values from -0.25 to 0.25
- self_qkv: bfloat16 [1024, 1536], replicated, may hold values from -0.1875 to 0.1875
- self_out: bfloat16 [512, 1024], replicated, may hold values from -0.25 to 0.25
- write_query: bfloat16 [1024, 512], replicated, may hold values from -0.1875 to 0.1875
- write_keyval: bfloat16 [1024, 1024], replicated, may hold values from -0.1875 to 0.1875
- write_out: bfloat16 [512, 1024], replicated, may hold values from -0.25 to 0.25
- qk_gain: float32 [6, 512], replicated, may hold values from 0.8 to 2.2
Outputs:
- tokens_out: bfloat16 [6144, 1024], P(('ba', 'aa')), parts along dimension 0
- latents_out: bfloat16 [1024, 1024], P(('ba', 'aa')), parts along dimension 0
The draws below stay inside these ranges and needn't reach their ends.
There are 4 independent parts, one for each index of `ba`. The reference program is written for one: setup_inputs(seed, part) draws one part's arguments, and reference() takes and returns one part's arrays. A program takes and returns all parts, laid end to end along the dimension named above; an argument that names none is the same for every part. Nothing has to cross between parts.
All inputs are finite; a program needn't handle non-finite values.
Results may differ from the reference program's by a relative error of at most 0.014.
Values may be sent and summed in bfloat16 or wider, within the bound.
A program may use at most 64 MiB of HBM per device.

```python
import math
import jax
import jax.numpy as jnp
from jax import lax

D = 1024
HEADS = 8
INNER = 512
TOKENS = 1536
LATENTS = 256


def steps_of(own_key, extent, cuts, smallest, largest):
    def one(position, parts):
        steps = jax.random.uniform(jax.random.fold_in(jax.random.fold_in(own_key, 6), position), (parts,), jnp.float32, smallest / len(cuts), largest / len(cuts))
        return jnp.repeat(jnp.exp(steps), extent[position] // parts).reshape((-1,) + (1,) * (len(extent) - position - 1))

    factor_of = one(*cuts[0])
    for cut in cuts[1:]:
        factor_of = factor_of * one(*cut)
    return factor_of


def normal_values(key, extent, width, limit, cuts=(), kind=jnp.bfloat16):
    loudness = steps_of(key, extent, cuts, -0.22, 0.18) if cuts else 1.0
    values = jax.random.normal(key, extent, jnp.float32) * width * loudness
    return jnp.minimum(jnp.maximum(values, -limit), limit).astype(kind)


def setup_inputs(seed: int = 0, part: int = 0) -> dict:
    splits = jax.random.split(jax.random.key(seed), 12)
    own_keys = jax.random.split(jax.random.fold_in(splits[11], part), 12)
    tokens = normal_values(own_keys[0], (TOKENS, D), 1.0, 6.0, ((0, 8),))
    latents = normal_values(own_keys[1], (LATENTS, D), 1.0, 6.0, ((0, 8),))
    read_query = normal_values(splits[2], (D, INNER), D ** -0.5, 0.1875)
    read_keyval = normal_values(splits[3], (D, 2 * INNER), D ** -0.5, 0.1875)
    read_out = normal_values(splits[4], (INNER, D), INNER ** -0.5, 0.25)
    self_qkv = normal_values(splits[5], (D, 3 * INNER), D ** -0.5, 0.1875)
    self_out = normal_values(splits[6], (INNER, D), INNER ** -0.5, 0.25)
    write_query = normal_values(splits[7], (D, INNER), D ** -0.5, 0.1875)
    write_keyval = normal_values(splits[8], (D, 2 * INNER), D ** -0.5, 0.1875)
    write_out = normal_values(splits[9], (INNER, D), INNER ** -0.5, 0.25)
    qk_gain = jnp.clip(jnp.exp(jax.random.uniform(splits[10], (6, INNER), jnp.float32, math.log(0.8), math.log(2.2))), 0.8, 2.2)
    return {"tokens": tokens, "latents": latents, "read_query": read_query, "read_keyval": read_keyval, "read_out": read_out, "self_qkv": self_qkv, "self_out": self_out, "write_query": write_query, "write_keyval": write_keyval, "write_out": write_out, "qk_gain": qk_gain}


EPSILON = 1e-06

def rms_rows(values):
    widened = values.astype(jnp.float32)
    return (widened * lax.rsqrt(lax.optimization_barrier(jnp.mean(widened * widened, axis=-1, keepdims=True)) + EPSILON)).astype(jnp.bfloat16)

def head_norm(projected, gain_row, head_count):
    row_count = projected.shape[0]
    split_heads = projected.reshape(row_count, head_count, -1)
    normed = split_heads * lax.rsqrt(lax.optimization_barrier(jnp.mean(split_heads * split_heads, axis=-1, keepdims=True)) + EPSILON)
    return (normed.reshape(row_count, -1) * gain_row).astype(jnp.bfloat16)

def attend_block(query_rows, key_rows, value_rows, head_count):
    row_count = query_rows.shape[0]
    query_heads = query_rows.reshape(row_count, head_count, -1).astype(jnp.float32)
    key_heads = key_rows.reshape(key_rows.shape[0], head_count, -1).astype(jnp.float32)
    value_heads = value_rows.reshape(value_rows.shape[0], head_count, -1).astype(jnp.float32)
    score_scale = 1.0 / math.sqrt(query_heads.shape[2])
    scores = jnp.einsum('qhe,khe->hqk', query_heads, key_heads) * score_scale
    weights = jnp.exp(scores)
    denominator = lax.optimization_barrier(jnp.sum(weights, axis=2)).T
    rounded = lax.optimization_barrier(weights.astype(jnp.bfloat16)).astype(jnp.float32)
    numerator = jnp.einsum('hqk,khe->qhe', rounded, value_heads)
    quotient = numerator / denominator[:, :, None]
    return quotient.reshape(row_count, -1).astype(jnp.bfloat16)

def attention(query_rows, key_rows, value_rows, head_count):
    row_count = query_rows.shape[0]
    if row_count > 512 and row_count % 512 == 0:
        blocks = query_rows.reshape(row_count // 512, 512, query_rows.shape[1])
        result = lax.map(lambda one_block: attend_block(one_block, key_rows, value_rows, head_count), blocks)
        return result.reshape(row_count, -1)
    return attend_block(query_rows, key_rows, value_rows, head_count)

def residual_add(base, attended, projection):
    update = jnp.dot(attended, projection, preferred_element_type=jnp.float32)
    return (base.astype(jnp.float32) + update).astype(jnp.bfloat16)

def reference(tokens, latents, read_query, read_keyval, read_out, self_qkv, self_out, write_query, write_keyval, write_out, qk_gain):
    inner_width = read_query.shape[1]
    normed_tokens = rms_rows(tokens)
    normed_latents = rms_rows(latents)
    read_queries = head_norm(jnp.dot(normed_latents, read_query, preferred_element_type=jnp.float32), qk_gain[0], HEADS)
    token_pairs = jnp.dot(normed_tokens, read_keyval, preferred_element_type=jnp.float32)
    read_keys = head_norm(token_pairs[:, :inner_width], qk_gain[1], HEADS)
    read_values = token_pairs[:, inner_width:].astype(jnp.bfloat16)
    read_attended = attention(read_queries, read_keys, read_values, HEADS)
    read_latents = residual_add(latents, read_attended, read_out)
    self_normed = rms_rows(read_latents)
    triple = jnp.dot(self_normed, self_qkv, preferred_element_type=jnp.float32)
    self_queries = head_norm(triple[:, :inner_width], qk_gain[2], HEADS)
    self_keys = head_norm(triple[:, inner_width:2 * inner_width], qk_gain[3], HEADS)
    self_values = triple[:, 2 * inner_width:].astype(jnp.bfloat16)
    self_attended = attention(self_queries, self_keys, self_values, HEADS)
    latents_out = residual_add(read_latents, self_attended, self_out)
    write_queries = head_norm(jnp.dot(normed_tokens, write_query, preferred_element_type=jnp.float32), qk_gain[4], HEADS)
    write_normed = rms_rows(latents_out)
    latent_pairs = jnp.dot(write_normed, write_keyval, preferred_element_type=jnp.float32)
    write_keys = head_norm(latent_pairs[:, :inner_width], qk_gain[5], HEADS)
    write_values = latent_pairs[:, inner_width:].astype(jnp.bfloat16)
    write_attended = attention(write_queries, write_keys, write_values, HEADS)
    tokens_out = residual_add(tokens, write_attended, write_out)
    return (tokens_out, latents_out)
```

```python
import functools
import math

import jax
import jax.numpy as jnp
from jax import lax
from jax.experimental import pallas as pl
from jax.experimental.pallas import tpu as pltpu
from jax.sharding import PartitionSpec as P

HEADS = 8
EPSILON = 1e-06
MESH = pl.DeviceIdType.MESH
TILE = 256
LANES = 128
F32 = jnp.float32
BF16 = jnp.bfloat16


def dot(a, b):
    return jnp.dot(a, b, preferred_element_type=F32)


def dot_nt(a, b):
    return lax.dot_general(a, b, (((1,), (1,)), ((), ())), preferred_element_type=F32)


def rms(x):
    x = x.astype(F32)
    return (x * lax.rsqrt(jnp.mean(x * x, axis=-1, keepdims=True) + EPSILON)).astype(BF16)


def row_blocks(rows, body):
    block = min(rows, TILE)
    if rows == block:
        body(pl.ds(0, block))
    else:

        def step(i, carry):
            body(pl.ds(pl.multiple_of(i * block, block), block))
            return carry

        lax.fori_loop(0, rows // block, step, 0)


def kernel(
    n,
    tokens,
    latents,
    w_rq,
    w_rkv,
    w_ro,
    w_sqkv,
    w_so,
    w_wq,
    w_wkv,
    w_wo,
    gain,
    tok_out,
    lat_out,
    tok,
    lat_all,
    b_rq,
    b_rkv,
    b_ro,
    b_sqkv,
    b_so,
    b_wq,
    b_wkv,
    b_wo,
    ntok,
    rk,
    rv,
    wq,
    rq,
    part,
    recv,
    att,
    rlat,
    normed,
    sq,
    sk,
    sv,
    wk,
    wv,
    mean_mat,
    load_sem,
    send_sem,
    recv_sem,
):
    me = lax.axis_index("aa")
    own = latents.shape[0]
    every = n * own
    inner = w_rq.shape[1]
    width = inner // HEADS
    tiles = inner // TILE
    d = tokens.shape[1]
    pairs = inner // LANES

    mine = pl.ds(pl.multiple_of(me * own, own), own)
    loads = []
    order = (
        (latents, lat_all.at[mine]),
        (tokens, tok),
        (w_rkv, b_rkv),
        (w_rq, b_rq),
        (w_wq, b_wq),
        (w_ro, b_ro),
        (w_sqkv, b_sqkv),
        (w_so, b_so),
        (w_wkv, b_wkv),
        (w_wo, b_wo),
    )
    for i, (src, dst) in enumerate(order):
        copy = pltpu.make_async_copy(src, dst, load_sem.at[i])
        copy.start()
        loads.append(copy)
    l_lat, l_tok, l_rkv, l_rq, l_wq, l_ro, l_sqkv, l_so, l_wkv, l_wo = loads

    barrier = pltpu.get_barrier_semaphore()
    peers = [lax.rem(me + k, n) for k in range(1, n)]
    for peer in peers:
        pl.semaphore_signal(barrier, inc=1, device_id={"aa": peer}, device_id_type=MESH)

    row = lax.broadcasted_iota(jnp.int32, (TILE, TILE), 0) // width
    col = lax.broadcasted_iota(jnp.int32, (TILE, TILE), 1) // width
    mean_mat[...] = jnp.where(row == col, 1.0 / width, 0.0).astype(BF16)

    pl.semaphore_wait(barrier, n - 1)

    def remote(stage, k, src, dst):
        return pltpu.make_async_remote_copy(
            src_ref=src,
            dst_ref=dst,
            send_sem=send_sem.at[stage, k],
            recv_sem=recv_sem.at[stage, k],
            device_id={"aa": peers[k]},
            device_id_type=MESH,
        )

    gather_lat = [remote(0, k, latents, lat_all.at[mine]) for k in range(n - 1)]
    for copy in gather_lat:
        copy.start()

    def head_norm(y, index, tile, scale=None):
        mean = dot((y * y).astype(BF16), mean_mat[...])
        g = gain[index : index + 1, tile * TILE : (tile + 1) * TILE]
        if scale is not None:
            g = g * scale
        return (y * lax.rsqrt(mean + EPSILON) * g).astype(BF16)

    to_exp2 = math.log2(math.e) / math.sqrt(width)
    lane = lax.broadcasted_iota(jnp.int32, (1, LANES), 1)
    even = (lane < width).astype(F32)
    even_b, odd_b = even.astype(BF16), (1.0 - even).astype(BF16)

    def pair_attend(q, k, v):
        v1 = jnp.concatenate([v, jnp.ones_like(v)], axis=1)
        outs = []
        for mask in (even_b, odd_b):
            weights = jnp.exp2(dot_nt(q * mask, k)).astype(BF16)
            outs.append(dot(weights, v1))
        return outs

    def attend_into(q_ref, k_ref, v_ref, rows):
        pieces = []
        for p in range(pairs):
            cols = slice(p * LANES, (p + 1) * LANES)
            first, second = pair_attend(q_ref[rows, cols], k_ref[:, cols], v_ref[:, cols])
            num = jnp.where(lane < width, first[:, :LANES], second[:, :LANES])
            den = jnp.where(lane < width, first[:, LANES:], second[:, LANES:])
            pieces.append((num / den).astype(BF16))
        return jnp.concatenate(pieces, axis=1)

    l_tok.wait()
    ntok[...] = rms(tok[...])
    l_rkv.wait()
    for t in range(tiles):
        cols = slice(t * TILE, (t + 1) * TILE)
        rk[:, cols] = head_norm(dot(ntok[...], b_rkv[:, cols]), 1, t)
        vcols = slice(inner + t * TILE, inner + (t + 1) * TILE)
        rv[:, cols] = dot(ntok[...], b_rkv[:, vcols]).astype(BF16)

    l_lat.wait()
    l_rq.wait()
    for copy in gather_lat:
        copy.wait_recv()

    def read_queries(rows):
        normed[rows, :] = rms(lat_all[rows, :])
        for t in range(tiles):
            cols = slice(t * TILE, (t + 1) * TILE)
            rq[rows, cols] = head_norm(dot(normed[rows, :], b_rq[:, cols]), 0, t, to_exp2)

    row_blocks(every, read_queries)

    spread = LANES // HEADS

    def read_partial(rows):
        dens = None
        for p in range(pairs):
            cols = slice(p * LANES, (p + 1) * LANES)
            first, second = pair_attend(rq[rows, cols], rk[:, cols], rv[:, cols])
            part[rows, cols] = jnp.where(
                lane < width, first[:, :LANES], second[:, :LANES]
            ).astype(BF16)
            for j, one in enumerate((first, second)):
                head = 2 * p + j
                den = one[:, LANES:]
                dens = den if dens is None else jnp.where(lane >= head * spread, den, dens)
        part[rows, inner:] = dens.astype(BF16)

    row_blocks(every, read_partial)

    scatter = []
    for k in range(n - 1):
        theirs = pl.ds(pl.multiple_of(peers[k] * own, own), own)
        scatter.append(remote(1, k, part.at[theirs], recv.at[k]))
    for copy in scatter:
        copy.start()

    l_wq.wait()
    for t in range(tiles):
        cols = slice(t * TILE, (t + 1) * TILE)
        wq[:, cols] = head_norm(dot(ntok[...], b_wq[:, cols]), 4, t, to_exp2)

    pick_row = lax.broadcasted_iota(jnp.int32, (LANES, inner), 0)
    pick_col = lax.broadcasted_iota(jnp.int32, (LANES, inner), 1)
    pick = jnp.where(pick_row == (pick_col // width) * spread, 1.0, 0.0).astype(BF16)

    total = part[mine, :].astype(F32)
    for k in range(n - 1):
        scatter[k].wait_recv()
        total = total + recv[k].astype(F32)
    den = total[:, inner:]
    high = den.astype(BF16)
    low = (den - high.astype(F32)).astype(BF16)
    den = dot(high, pick) + dot(low, pick)
    att[mine, :] = (total[:, :inner] / den).astype(BF16)

    gather_att = [remote(2, k, att.at[mine], att.at[mine]) for k in range(n - 1)]
    for copy in gather_att:
        copy.start()

    l_ro.wait()
    l_sqkv.wait()
    for copy in gather_att:
        copy.wait_recv()

    def self_project(rows):
        new = lat_all[rows, :].astype(F32) + dot(att[rows, :], b_ro[...])
        new = new.astype(BF16)
        rlat[rows, :] = new
        normed[rows, :] = rms(new)
        for t in range(tiles):
            cols = slice(t * TILE, (t + 1) * TILE)
            for which, (ref, index, scale) in enumerate(
                ((sq, 2, to_exp2), (sk, 3, None), (sv, None, None))
            ):
                start = which * inner + t * TILE
                y = dot(normed[rows, :], b_sqkv[:, start : start + TILE])
                ref[rows, cols] = (
                    y.astype(BF16) if index is None else head_norm(y, index, t, scale)
                )

    row_blocks(every, self_project)

    l_so.wait()
    l_wkv.wait()

    def self_attend(rows):
        attended = attend_into(sq, sk, sv, rows)
        new = rlat[rows, :].astype(F32) + dot(attended, b_so[...])
        new = new.astype(BF16)
        rlat[rows, :] = new
        normed[rows, :] = rms(new)
        for t in range(tiles):
            cols = slice(t * TILE, (t + 1) * TILE)
            wk[rows, cols] = head_norm(dot(normed[rows, :], b_wkv[:, cols]), 5, t)
            vcols = slice(inner + t * TILE, inner + (t + 1) * TILE)
            wv[rows, cols] = dot(normed[rows, :], b_wkv[:, vcols]).astype(BF16)

    row_blocks(every, self_attend)
    lat_out[...] = rlat[mine, :]

    l_wo.wait()
    attended = attend_into(wq, wk, wv, slice(None))
    tok_out[...] = (tok[...].astype(F32) + dot(attended, b_wo[...])).astype(BF16)

    for copy in gather_lat + scatter + gather_att:
        copy.wait_send()


def per_device(n, tokens, latents, *weights_and_gain):
    weights, gain = weights_and_gain[:-1], weights_and_gain[-1]
    own, d = latents.shape
    count = tokens.shape[0]
    inner = weights[0].shape[1]
    every = n * own
    hbm = pl.BlockSpec(memory_space=pl.ANY)
    vmem = pl.BlockSpec(memory_space=pltpu.VMEM)

    def buf(*shape):
        return pltpu.VMEM(shape, BF16)

    return pl.pallas_call(
        functools.partial(kernel, n),
        out_shape=(
            jax.ShapeDtypeStruct(tokens.shape, BF16),
            jax.ShapeDtypeStruct(latents.shape, BF16),
        ),
        in_specs=[hbm] * 10 + [vmem],
        out_specs=(vmem, vmem),
        scratch_shapes=[
            buf(count, d),
            buf(every, d),
            *[buf(*w.shape) for w in weights],
            buf(count, d),
            buf(count, inner),
            buf(count, inner),
            buf(count, inner),
            buf(every, inner),
            buf(every, inner + LANES),
            buf(n - 1, own, inner + LANES),
            buf(every, inner),
            buf(every, d),
            buf(every, d),
            *[buf(every, inner) for _ in range(5)],
            buf(TILE, TILE),
            pltpu.SemaphoreType.DMA((10,)),
            pltpu.SemaphoreType.DMA((3, n - 1)),
            pltpu.SemaphoreType.DMA((3, n - 1)),
        ],
        compiler_params=pltpu.CompilerParams(
            collective_id=0, has_side_effects=True, vmem_limit_bytes=60 * 1024 * 1024
        ),
        name="rin_block",
    )(tokens, latents, *weights, gain)


def solution(mesh):
    rows = P(("ba", "aa"), None)
    return jax.shard_map(
        functools.partial(per_device, mesh.shape["aa"]),
        mesh=mesh,
        in_specs=(rows, rows) + (P(),) * 9,
        out_specs=(rows, rows),
        check_vma=False,
    )
```

```python
import functools
import math

import jax
import jax.numpy as jnp
from jax import lax
from jax.experimental import pallas as pl
from jax.experimental.pallas import tpu as pltpu
from jax.sharding import PartitionSpec as P

HEADS = 8
EPSILON = 1e-06
MESH = pl.DeviceIdType.MESH
TILE = 256
LANES = 128
F32 = jnp.float32
BF16 = jnp.bfloat16


def dot(a, b):
    return jnp.dot(a, b, preferred_element_type=F32)


def dot_nt(a, b):
    return lax.dot_general(a, b, (((1,), (1,)), ((), ())), preferred_element_type=F32)


def rms(x):
    x = x.astype(F32)
    return (x * lax.rsqrt(jnp.mean(x * x, axis=-1, keepdims=True) + EPSILON)).astype(BF16)


def row_blocks(rows, body):
    block = min(rows, TILE)
    if rows == block:
        body(pl.ds(0, block))
    else:

        def step(i, carry):
            body(pl.ds(pl.multiple_of(i * block, block), block))
            return carry

        lax.fori_loop(0, rows // block, step, 0)


def kernel(
    n,
    tokens,
    latents,
    w_rq,
    w_rkv,
    w_ro,
    w_sqkv,
    w_so,
    w_wq,
    w_wkv,
    w_wo,
    gain,
    tok_out,
    lat_out,
    tok,
    lat_all,
    b_rq,
    b_rkv,
    b_ro,
    b_sqkv,
    b_so,
    b_wq,
    b_wkv,
    b_wo,
    ntok,
    wq,
    q_send,
    q_all,
    kv_send,
    kv_all,
    heads_all,
    att,
    rlat,
    normed,
    sq,
    sk,
    sv,
    wk,
    wv,
    mean_mat,
    load_sem,
    send_sem,
    recv_sem,
):
    me = lax.axis_index("aa")
    own = latents.shape[0]
    every = n * own
    inner = w_rq.shape[1]
    width = inner // HEADS
    tiles = inner // TILE
    d = tokens.shape[1]
    pairs = inner // LANES

    count = tokens.shape[0]
    share = n // HEADS
    block = every // share
    half = block // 2
    chips = n // 2
    my_head = me // share

    barrier = pltpu.get_barrier_semaphore()
    peers = [lax.rem(me + k, n) for k in range(1, n)]
    sources = [lax.rem(me + n - k, n) for k in range(1, n)]
    partner = me + 1 - 2 * lax.rem(me, 2)
    for peer in peers:
        pl.semaphore_signal(barrier, inc=1, device_id={"aa": peer}, device_id_type=MESH)

    def rows_of(device, size):
        return pl.ds(pl.multiple_of(device * size, size), size)

    mine = rows_of(me, own)
    loads = []
    order = (
        (latents, lat_all.at[mine]),
        (w_rq, b_rq),
        (tokens, tok),
        (w_rkv, b_rkv),
        (w_wq, b_wq),
        (w_ro, b_ro),
        (w_sqkv, b_sqkv),
        (w_so, b_so),
        (w_wkv, b_wkv),
        (w_wo, b_wo),
    )
    for i, (src, dst) in enumerate(order):
        copy = pltpu.make_async_copy(src, dst, load_sem.at[i])
        copy.start()
        loads.append(copy)
    l_lat, l_rq, l_tok, l_rkv, l_wq, l_ro, l_sqkv, l_so, l_wkv, l_wo = loads

    row = lax.broadcasted_iota(jnp.int32, (TILE, TILE), 0) // width
    col = lax.broadcasted_iota(jnp.int32, (TILE, TILE), 1) // width
    mean_mat[...] = jnp.where(row == col, 1.0 / width, 0.0).astype(BF16)

    def remote(stage, k, src, dst, device):
        return pltpu.make_async_remote_copy(
            src_ref=src,
            dst_ref=dst,
            send_sem=send_sem.at[stage, k],
            recv_sem=recv_sem.at[stage, k],
            device_id={"aa": device},
            device_id_type=MESH,
        )

    def head_norm(y, index, tile, scale=None):
        mean = dot((y * y).astype(BF16), mean_mat[...])
        g = gain[index : index + 1, tile * TILE : (tile + 1) * TILE]
        if scale is not None:
            g = g * scale
        return y * lax.rsqrt(mean + EPSILON) * g

    to_exp2 = math.log2(math.e) / math.sqrt(width)
    lane = lax.broadcasted_iota(jnp.int32, (1, LANES), 1)
    low = lane < width
    even_b = low.astype(F32).astype(BF16)
    odd_b = (1.0 - low.astype(F32)).astype(BF16)
    per_tile = TILE // LANES

    def pair_attend(q, k, v):
        v1 = jnp.concatenate([v, jnp.ones_like(v)], axis=1)
        outs = []
        for mask in (even_b, odd_b):
            weights = jnp.exp2(dot_nt(q * mask, k)).astype(BF16)
            outs.append(dot(weights, v1))
        return outs

    def attend_into(q_ref, k_ref, v_ref, rows):
        pieces = []
        for p in range(pairs):
            cols = slice(p * LANES, (p + 1) * LANES)
            first, second = pair_attend(q_ref[rows, cols], k_ref[:, cols], v_ref[:, cols])
            num = jnp.where(low, first[:, :LANES], second[:, :LANES])
            den = jnp.where(low, first[:, LANES:], second[:, LANES:])
            pieces.append((num / den).astype(BF16))
        return jnp.concatenate(pieces, axis=1)

    l_lat.wait()
    l_rq.wait()
    own_normed = rms(lat_all[mine, :])
    for t in range(tiles):
        cols = slice(t * TILE, (t + 1) * TILE)
        q = head_norm(dot(own_normed, b_rq[:, cols]), 0, t, to_exp2).astype(BF16)
        for j in range(per_tile):
            q_send[t * per_tile + j] = q[:, j * LANES : (j + 1) * LANES]
    q_all[mine, :] = q_send[my_head // 2]

    pl.semaphore_wait(barrier, n - 1)

    send_q = [
        remote(0, k, q_send.at[peers[k] // (2 * share)], q_all.at[mine], peers[k])
        for k in range(n - 1)
    ]
    for copy in send_q:
        copy.start()

    l_tok.wait()
    ntok[...] = rms(tok[...])
    l_rkv.wait()
    for t in range(tiles):
        cols = slice(t * TILE, (t + 1) * TILE)
        vcols = slice(inner + t * TILE, inner + (t + 1) * TILE)
        keys = head_norm(dot(ntok[...], b_rkv[:, cols]), 1, t)
        values = dot(ntok[...], b_rkv[:, vcols])
        for j in range(per_tile):
            part = slice(j * LANES, (j + 1) * LANES)
            k, v = keys[:, part], pltpu.roll(values[:, part], width, 1)
            head = 2 * (t * per_tile + j)
            kv_send[head] = jnp.where(low, k, v).astype(BF16)
            kv_send[head + 1] = jnp.where(low, v, k).astype(BF16)
    my_tokens = rows_of(me, count)
    send_kv = [
        remote(1, k, kv_send.at[peers[k] // share], kv_all.at[my_tokens], peers[k])
        for k in range(n - 1)
    ]
    for copy in send_kv:
        copy.start()
    kv_all[my_tokens, :] = kv_send[my_head]

    send_lat = [
        remote(2, j - 1, latents, lat_all.at[mine], lax.rem(me + 2 * j, n))
        for j in range(1, chips)
    ]
    send_lat.append(remote(2, chips - 1, latents, lat_all.at[mine], partner))
    for copy in send_lat:
        copy.start()

    l_wq.wait()
    for t in range(tiles):
        cols = slice(t * TILE, (t + 1) * TILE)
        wq[:, cols] = head_norm(dot(ntok[...], b_wq[:, cols]), 4, t, to_exp2).astype(BF16)

    for copy in send_q:
        copy.wait_recv()
    parity = lax.rem(my_head, 2)
    mine_b = jnp.where(lane // width == parity, 1.0, 0.0).astype(BF16)
    q = q_all[rows_of(lax.rem(me, share), block), :] * mine_b
    total = None
    for k in range(n):
        if k:
            send_kv[k - 1].wait_recv()
        kv = kv_all[rows_of(sources[k - 1] if k else me, count), :]
        weights = jnp.exp2(dot_nt(q, kv)).astype(BF16)
        term = dot(weights, jnp.concatenate([kv, jnp.ones_like(kv)], axis=1))
        total = term if total is None else total + term
    quotient = total[:, :LANES] / total[:, LANES:]
    message = jnp.where(
        lane // width == parity, pltpu.roll(quotient[:half], width, 1), quotient[half:]
    )
    heads_all[me] = message.astype(BF16)
    gather_att = [
        remote(3, k, heads_all.at[me], heads_all.at[me], peers[k]) for k in range(n - 1)
    ]
    for copy in gather_att:
        copy.start()

    relay_lat = []
    for j in range(1, chips):
        send_lat[j - 1].wait_recv()
        theirs = rows_of(lax.rem(me + n - 2 * j, n), own)
        copy = remote(2, chips - 1 + j, lat_all.at[theirs], lat_all.at[theirs], partner)
        copy.start()
        relay_lat.append(copy)
    send_lat[chips - 1].wait_recv()
    for copy in relay_lat:
        copy.wait_recv()

    l_ro.wait()
    l_sqkv.wait()
    for copy in gather_att:
        copy.wait_recv()
    for p in range(pairs):
        cols = slice(p * LANES, (p + 1) * LANES)
        for b in range(share):
            first = heads_all[2 * p * share + b].astype(F32)
            second = heads_all[(2 * p + 1) * share + b].astype(F32)
            top = jnp.where(low, first, second)
            bottom = pltpu.roll(jnp.where(low, second, first), width, 1)
            att[b * block : b * block + half, cols] = top.astype(BF16)
            att[b * block + half : (b + 1) * block, cols] = bottom.astype(BF16)

    def self_project(rows):
        new = lat_all[rows, :].astype(F32) + dot(att[rows, :], b_ro[...])
        new = new.astype(BF16)
        rlat[rows, :] = new
        normed[rows, :] = rms(new)
        for t in range(tiles):
            cols = slice(t * TILE, (t + 1) * TILE)
            for which, (ref, index, scale) in enumerate(
                ((sq, 2, to_exp2), (sk, 3, None), (sv, None, None))
            ):
                start = which * inner + t * TILE
                y = dot(normed[rows, :], b_sqkv[:, start : start + TILE])
                y = y if index is None else head_norm(y, index, t, scale)
                ref[rows, cols] = y.astype(BF16)

    row_blocks(every, self_project)

    l_so.wait()
    l_wkv.wait()

    def self_attend(rows):
        attended = attend_into(sq, sk, sv, rows)
        new = rlat[rows, :].astype(F32) + dot(attended, b_so[...])
        new = new.astype(BF16)
        rlat[rows, :] = new
        normed[rows, :] = rms(new)
        for t in range(tiles):
            cols = slice(t * TILE, (t + 1) * TILE)
            wk[rows, cols] = head_norm(dot(normed[rows, :], b_wkv[:, cols]), 5, t).astype(BF16)
            vcols = slice(inner + t * TILE, inner + (t + 1) * TILE)
            wv[rows, cols] = dot(normed[rows, :], b_wkv[:, vcols]).astype(BF16)

    row_blocks(every, self_attend)
    lat_out[...] = rlat[mine, :]

    l_wo.wait()
    attended = attend_into(wq, wk, wv, slice(None))
    tok_out[...] = (tok[...].astype(F32) + dot(attended, b_wo[...])).astype(BF16)

    for copy in send_q + send_kv + send_lat + relay_lat + gather_att:
        copy.wait_send()


def per_device(n, tokens, latents, *weights_and_gain):
    weights, gain = weights_and_gain[:-1], weights_and_gain[-1]
    own, d = latents.shape
    count = tokens.shape[0]
    inner = weights[0].shape[1]
    every = n * own
    hbm = pl.BlockSpec(memory_space=pl.ANY)
    vmem = pl.BlockSpec(memory_space=pltpu.VMEM)

    def buf(*shape):
        return pltpu.VMEM(shape, BF16)

    return pl.pallas_call(
        functools.partial(kernel, n),
        out_shape=(
            pltpu.VMEM(tokens.shape, BF16),
            pltpu.VMEM(latents.shape, BF16),
        ),
        in_specs=[hbm] * 10 + [vmem],
        out_specs=(vmem, vmem),
        scratch_shapes=[
            buf(count, d),
            buf(every, d),
            *[buf(*w.shape) for w in weights],
            buf(count, d),
            buf(count, inner),
            buf(inner // LANES, own, LANES),
            buf(every, LANES),
            buf(HEADS, count, LANES),
            buf(n * count, LANES),
            buf(n, every * HEADS // n // 2, LANES),
            buf(every, inner),
            buf(every, d),
            buf(every, d),
            *[buf(every, inner) for _ in range(5)],
            buf(TILE, TILE),
            pltpu.SemaphoreType.DMA((10,)),
            pltpu.SemaphoreType.DMA((4, n - 1)),
            pltpu.SemaphoreType.DMA((4, n - 1)),
        ],
        compiler_params=pltpu.CompilerParams(
            collective_id=0, has_side_effects=True, vmem_limit_bytes=67043328 - 1000 * 1024
        ),
        name="rin_block",
    )(tokens, latents, *weights, gain)


def solution(mesh):
    rows = P(("ba", "aa"), None)
    return jax.shard_map(
        functools.partial(per_device, mesh.shape["aa"]),
        mesh=mesh,
        in_specs=(rows, rows) + (P(),) * 9,
        out_specs=(rows, rows),
        check_vma=False,
    )
```

```python
import functools
import math

import jax
import jax.numpy as jnp
from jax import lax
from jax.experimental import pallas as pl
from jax.experimental.pallas import tpu as pltpu
from jax.sharding import PartitionSpec as P

HEADS = 8
EPSILON = 1e-06
MESH = pl.DeviceIdType.MESH
TILE = 256
LANES = 128
F32 = jnp.float32
BF16 = jnp.bfloat16


def dot(a, b):
    return jnp.dot(a, b, preferred_element_type=F32)


def dot_nt(a, b):
    return lax.dot_general(a, b, (((1,), (1,)), ((), ())), preferred_element_type=F32)


def rms(x):
    x = x.astype(F32)
    return (x * lax.rsqrt(jnp.mean(x * x, axis=-1, keepdims=True) + EPSILON)).astype(BF16)


def row_blocks(rows, body):
    block = min(rows, TILE)
    if rows == block:
        body(pl.ds(0, block))
    else:

        def step(i, carry):
            body(pl.ds(pl.multiple_of(i * block, block), block))
            return carry

        lax.fori_loop(0, rows // block, step, 0)


def kernel(
    n,
    tokens,
    latents,
    w_rq,
    w_rkv,
    w_ro,
    w_sqkv,
    w_so,
    w_wq,
    w_wkv,
    w_wo,
    gain,
    tok_out,
    lat_out,
    tok,
    lat_all,
    b_rq,
    b_rkv,
    b_ro,
    b_sqkv,
    b_so,
    b_wq,
    b_wkv,
    b_wo,
    ntok,
    wq,
    q_send,
    q_all,
    kv_send,
    kv_all,
    heads_all,
    att,
    rlat,
    normed,
    sq,
    sk,
    sv,
    wk,
    wv,
    mean_mat,
    load_sem,
    send_sem,
    recv_sem,
):
    me = lax.axis_index("aa")
    own = latents.shape[0]
    every = n * own
    inner = w_rq.shape[1]
    width = inner // HEADS
    tiles = inner // TILE
    d = tokens.shape[1]
    pairs = inner // LANES

    count = tokens.shape[0]
    share = n // HEADS
    block = every // share
    half = block // 2
    chips = n // 2
    my_head = me // share

    barrier = pltpu.get_barrier_semaphore()
    peers = [lax.rem(me + k, n) for k in range(1, n)]
    sources = [lax.rem(me + n - k, n) for k in range(1, n)]
    partner = me + 1 - 2 * lax.rem(me, 2)
    for peer in peers:
        pl.semaphore_signal(barrier, inc=1, device_id={"aa": peer}, device_id_type=MESH)

    def rows_of(device, size):
        return pl.ds(pl.multiple_of(device * size, size), size)

    mine = rows_of(me, own)
    loads = []
    order = (
        (latents, lat_all.at[mine]),
        (w_rq, b_rq),
        (tokens, tok),
        (w_rkv, b_rkv),
        (w_wq, b_wq),
        (w_ro, b_ro),
        (w_sqkv, b_sqkv),
        (w_so, b_so),
        (w_wkv, b_wkv),
        (w_wo, b_wo),
    )
    for i, (src, dst) in enumerate(order):
        copy = pltpu.make_async_copy(src, dst, load_sem.at[i])
        copy.start()
        loads.append(copy)
    l_lat, l_rq, l_tok, l_rkv, l_wq, l_ro, l_sqkv, l_so, l_wkv, l_wo = loads

    row = lax.broadcasted_iota(jnp.int32, (TILE, TILE), 0) // width
    col = lax.broadcasted_iota(jnp.int32, (TILE, TILE), 1) // width
    mean_mat[...] = jnp.where(row == col, 1.0 / width, 0.0).astype(BF16)

    def remote(stage, k, src, dst, device):
        return pltpu.make_async_remote_copy(
            src_ref=src,
            dst_ref=dst,
            send_sem=send_sem.at[stage, k],
            recv_sem=recv_sem.at[stage, k],
            device_id={"aa": device},
            device_id_type=MESH,
        )

    def head_norm(y, index, tile, scale=None):
        mean = dot((y * y).astype(BF16), mean_mat[...])
        g = gain[index : index + 1, tile * TILE : (tile + 1) * TILE]
        if scale is not None:
            g = g * scale
        return y * lax.rsqrt(mean + EPSILON) * g

    to_exp2 = math.log2(math.e) / math.sqrt(width)
    lane = lax.broadcasted_iota(jnp.int32, (1, LANES), 1)
    low = lane < width
    even_b = low.astype(F32).astype(BF16)
    odd_b = (1.0 - low.astype(F32)).astype(BF16)
    per_tile = TILE // LANES

    def pair_attend(q, k, v):
        v1 = jnp.concatenate([v, jnp.ones_like(v)], axis=1)
        outs = []
        for mask in (even_b, odd_b):
            weights = jnp.exp2(dot_nt(q * mask, k)).astype(BF16)
            outs.append(dot(weights, v1))
        return outs

    def attend_into(q_ref, k_ref, v_ref, rows):
        pieces = []
        for p in range(pairs):
            cols = slice(p * LANES, (p + 1) * LANES)
            first, second = pair_attend(q_ref[rows, cols], k_ref[:, cols], v_ref[:, cols])
            num = jnp.where(low, first[:, :LANES], second[:, :LANES])
            den = jnp.where(low, first[:, LANES:], second[:, LANES:])
            pieces.append((num / den).astype(BF16))
        return jnp.concatenate(pieces, axis=1)

    l_lat.wait()
    l_rq.wait()
    own_normed = rms(lat_all[mine, :])
    for t in range(tiles):
        cols = slice(t * TILE, (t + 1) * TILE)
        q = head_norm(dot(own_normed, b_rq[:, cols]), 0, t, to_exp2).astype(BF16)
        for j in range(per_tile):
            q_send[t * per_tile + j] = q[:, j * LANES : (j + 1) * LANES]
    q_all[mine, :] = q_send[my_head // 2]

    l_tok.wait()
    ntok[...] = rms(tok[...])
    l_rkv.wait()
    for t in range(tiles):
        cols = slice(t * TILE, (t + 1) * TILE)
        vcols = slice(inner + t * TILE, inner + (t + 1) * TILE)
        keys = head_norm(dot(ntok[...], b_rkv[:, cols]), 1, t)
        values = dot(ntok[...], b_rkv[:, vcols])
        for j in range(per_tile):
            part = slice(j * LANES, (j + 1) * LANES)
            k, v = keys[:, part], pltpu.roll(values[:, part], width, 1)
            head = 2 * (t * per_tile + j)
            kv_send[head] = jnp.where(low, k, v).astype(BF16)
            kv_send[head + 1] = jnp.where(low, v, k).astype(BF16)
    pl.semaphore_wait(barrier, n - 1)

    send_q = [
        remote(0, k, q_send.at[peers[k] // (2 * share)], q_all.at[mine], peers[k])
        for k in range(n - 1)
    ]
    for copy in send_q:
        copy.start()

    my_tokens = rows_of(me, count)
    send_kv = [
        remote(1, k, kv_send.at[peers[k] // share], kv_all.at[my_tokens], peers[k])
        for k in range(n - 1)
    ]
    for copy in send_kv:
        copy.start()
    kv_all[my_tokens, :] = kv_send[my_head]

    send_lat = [
        remote(2, j - 1, latents, lat_all.at[mine], lax.rem(me + 2 * j, n))
        for j in range(1, chips)
    ]
    send_lat.append(remote(2, chips - 1, latents, lat_all.at[mine], partner))
    for copy in send_lat:
        copy.start()

    l_wq.wait()
    for t in range(tiles):
        cols = slice(t * TILE, (t + 1) * TILE)
        wq[:, cols] = head_norm(dot(ntok[...], b_wq[:, cols]), 4, t, to_exp2).astype(BF16)

    for copy in send_q:
        copy.wait_recv()
    parity = lax.rem(my_head, 2)
    mine_b = jnp.where(lane // width == parity, 1.0, 0.0).astype(BF16)
    q = q_all[rows_of(lax.rem(me, share), block), :] * mine_b
    total = None
    for k in range(n):
        if k:
            send_kv[k - 1].wait_recv()
        kv = kv_all[rows_of(sources[k - 1] if k else me, count), :]
        weights = jnp.exp2(dot_nt(q, kv)).astype(BF16)
        term = dot(weights, jnp.concatenate([kv, jnp.ones_like(kv)], axis=1))
        total = term if total is None else total + term
    quotient = total[:, :LANES] / total[:, LANES:]
    message = jnp.where(
        lane // width == parity, pltpu.roll(quotient[:half], width, 1), quotient[half:]
    )
    heads_all[me] = message.astype(BF16)
    gather_att = [
        remote(3, k, heads_all.at[me], heads_all.at[me], peers[k]) for k in range(n - 1)
    ]
    for copy in gather_att:
        copy.start()

    relay_lat = []
    for j in range(1, chips):
        send_lat[j - 1].wait_recv()
        theirs = rows_of(lax.rem(me + n - 2 * j, n), own)
        copy = remote(2, chips - 1 + j, lat_all.at[theirs], lat_all.at[theirs], partner)
        copy.start()
        relay_lat.append(copy)
    send_lat[chips - 1].wait_recv()
    for copy in relay_lat:
        copy.wait_recv()

    l_ro.wait()
    l_sqkv.wait()
    for copy in gather_att:
        copy.wait_recv()
    for p in range(pairs):
        cols = slice(p * LANES, (p + 1) * LANES)
        for b in range(share):
            first = heads_all[2 * p * share + b].astype(F32)
            second = heads_all[(2 * p + 1) * share + b].astype(F32)
            top = jnp.where(low, first, second)
            bottom = pltpu.roll(jnp.where(low, second, first), width, 1)
            att[b * block : b * block + half, cols] = top.astype(BF16)
            att[b * block + half : (b + 1) * block, cols] = bottom.astype(BF16)

    def self_project(rows):
        new = lat_all[rows, :].astype(F32) + dot(att[rows, :], b_ro[...])
        new = new.astype(BF16)
        rlat[rows, :] = new
        normed[rows, :] = rms(new)
        for t in range(tiles):
            cols = slice(t * TILE, (t + 1) * TILE)
            for which, (ref, index, scale) in enumerate(
                ((sq, 2, to_exp2), (sk, 3, None), (sv, None, None))
            ):
                start = which * inner + t * TILE
                y = dot(normed[rows, :], b_sqkv[:, start : start + TILE])
                y = y if index is None else head_norm(y, index, t, scale)
                ref[rows, cols] = y.astype(BF16)

    row_blocks(every, self_project)

    l_so.wait()
    l_wkv.wait()

    def self_attend(rows):
        attended = attend_into(sq, sk, sv, rows)
        new = rlat[rows, :].astype(F32) + dot(attended, b_so[...])
        new = new.astype(BF16)
        rlat[rows, :] = new
        normed[rows, :] = rms(new)
        for t in range(tiles):
            cols = slice(t * TILE, (t + 1) * TILE)
            wk[rows, cols] = head_norm(dot(normed[rows, :], b_wkv[:, cols]), 5, t).astype(BF16)
            vcols = slice(inner + t * TILE, inner + (t + 1) * TILE)
            wv[rows, cols] = dot(normed[rows, :], b_wkv[:, vcols]).astype(BF16)

    row_blocks(every, self_attend)
    lat_out[...] = rlat[mine, :]

    l_wo.wait()
    attended = attend_into(wq, wk, wv, slice(None))
    tok_out[...] = (tok[...].astype(F32) + dot(attended, b_wo[...])).astype(BF16)

    for copy in send_q + send_kv + send_lat + relay_lat + gather_att:
        copy.wait_send()


def per_device(n, tokens, latents, *weights_and_gain):
    weights, gain = weights_and_gain[:-1], weights_and_gain[-1]
    own, d = latents.shape
    count = tokens.shape[0]
    inner = weights[0].shape[1]
    every = n * own
    hbm = pl.BlockSpec(memory_space=pl.ANY)
    vmem = pl.BlockSpec(memory_space=pltpu.VMEM)

    def buf(*shape):
        return pltpu.VMEM(shape, BF16)

    return pl.pallas_call(
        functools.partial(kernel, n),
        out_shape=(
            pltpu.VMEM(tokens.shape, BF16),
            pltpu.VMEM(latents.shape, BF16),
        ),
        in_specs=[hbm] * 10 + [vmem],
        out_specs=(vmem, vmem),
        scratch_shapes=[
            buf(count, d),
            buf(every, d),
            *[buf(*w.shape) for w in weights],
            buf(count, d),
            buf(count, inner),
            buf(inner // LANES, own, LANES),
            buf(every, LANES),
            buf(HEADS, count, LANES),
            buf(n * count, LANES),
            buf(n, every * HEADS // n // 2, LANES),
            buf(every, inner),
            buf(every, d),
            buf(every, d),
            *[buf(every, inner) for _ in range(5)],
            buf(TILE, TILE),
            pltpu.SemaphoreType.DMA((10,)),
            pltpu.SemaphoreType.DMA((4, n - 1)),
            pltpu.SemaphoreType.DMA((4, n - 1)),
        ],
        compiler_params=pltpu.CompilerParams(
            collective_id=0, has_side_effects=True, vmem_limit_bytes=67043328 - 1000 * 1024
        ),
        name="rin_block",
    )(tokens, latents, *weights, gain)


def solution(mesh):
    rows = P(("ba", "aa"), None)
    return jax.shard_map(
        functools.partial(per_device, mesh.shape["aa"]),
        mesh=mesh,
        in_specs=(rows, rows) + (P(),) * 9,
        out_specs=(rows, rows),
        check_vma=False,
    )
```

```python
import functools
import math

import jax
import jax.numpy as jnp
from jax import lax
from jax.experimental import pallas as pl
from jax.experimental.pallas import tpu as pltpu
from jax.sharding import PartitionSpec as P

HEADS = 8
EPSILON = 1e-06
MESH = pl.DeviceIdType.MESH
TILE = 256
LANES = 128
F32 = jnp.float32
BF16 = jnp.bfloat16


def dot(a, b):
    return jnp.dot(a, b, preferred_element_type=F32)


def dot_nt(a, b):
    return lax.dot_general(a, b, (((1,), (1,)), ((), ())), preferred_element_type=F32)


def rms(x):
    x = x.astype(F32)
    return (x * lax.rsqrt(jnp.mean(x * x, axis=-1, keepdims=True) + EPSILON)).astype(BF16)


def row_blocks(rows, body):
    block = min(rows, TILE)
    if rows == block:
        body(pl.ds(0, block))
    else:

        def step(i, carry):
            body(pl.ds(pl.multiple_of(i * block, block), block))
            return carry

        lax.fori_loop(0, rows // block, step, 0)


def kernel(
    n,
    tokens,
    latents,
    w_rq,
    w_rkv,
    w_ro,
    w_sqkv,
    w_so,
    w_wq,
    w_wkv,
    w_wo,
    gain,
    tok_out,
    lat_out,
    tok,
    lat_all,
    b_rq,
    b_rkv,
    b_ro,
    b_sqkv,
    b_so,
    b_wq,
    b_wkv,
    b_wo,
    ntok,
    wq,
    q_send,
    q_all,
    kv_send,
    kv_all,
    heads_all,
    att,
    rlat,
    normed,
    sq,
    sk,
    sv,
    wk,
    wv,
    mean_mat,
    load_sem,
    send_sem,
    recv_sem,
):
    me = lax.axis_index("aa")
    own = latents.shape[0]
    every = n * own
    inner = w_rq.shape[1]
    width = inner // HEADS
    tiles = inner // TILE
    d = tokens.shape[1]
    pairs = inner // LANES

    count = tokens.shape[0]
    share = n // HEADS
    block = every // share
    half = block // 2
    chips = n // 2
    my_head = me // share

    barrier = pltpu.get_barrier_semaphore()
    peers = [lax.rem(me + k, n) for k in range(1, n)]
    sources = [lax.rem(me + n - k, n) for k in range(1, n)]
    partner = me + 1 - 2 * lax.rem(me, 2)
    for peer in peers:
        pl.semaphore_signal(barrier, inc=1, device_id={"aa": peer}, device_id_type=MESH)

    def rows_of(device, size):
        return pl.ds(pl.multiple_of(device * size, size), size)

    mine = rows_of(me, own)
    loads = []
    order = (
        (latents, lat_all.at[mine]),
        (w_rq, b_rq),
        (tokens, tok),
        (w_rkv, b_rkv),
        (w_wq, b_wq),
        (w_ro, b_ro),
        (w_sqkv, b_sqkv),
        (w_so, b_so),
        (w_wkv, b_wkv),
        (w_wo, b_wo),
    )
    for i, (src, dst) in enumerate(order):
        copy = pltpu.make_async_copy(src, dst, load_sem.at[i])
        copy.start()
        loads.append(copy)
    l_lat, l_rq, l_tok, l_rkv, l_wq, l_ro, l_sqkv, l_so, l_wkv, l_wo = loads

    row = lax.broadcasted_iota(jnp.int32, (TILE, TILE), 0) // width
    col = lax.broadcasted_iota(jnp.int32, (TILE, TILE), 1) // width
    mean_mat[...] = jnp.where(row == col, 1.0 / width, 0.0).astype(BF16)

    def remote(stage, k, src, dst, device):
        return pltpu.make_async_remote_copy(
            src_ref=src,
            dst_ref=dst,
            send_sem=send_sem.at[stage, k],
            recv_sem=recv_sem.at[stage, k],
            device_id={"aa": device},
            device_id_type=MESH,
        )

    def head_norm(y, index, tile, scale=None):
        mean = dot((y * y).astype(BF16), mean_mat[...])
        g = gain[index : index + 1, tile * TILE : (tile + 1) * TILE]
        if scale is not None:
            g = g * scale
        return y * lax.rsqrt(mean + EPSILON) * g

    to_exp2 = math.log2(math.e) / math.sqrt(width)
    lane = lax.broadcasted_iota(jnp.int32, (1, LANES), 1)
    low = lane < width
    even_b = low.astype(F32).astype(BF16)
    odd_b = (1.0 - low.astype(F32)).astype(BF16)
    per_tile = TILE // LANES

    def pair_attend(q, k, v):
        v1 = jnp.concatenate([v, jnp.ones_like(v)], axis=1)
        outs = []
        for mask in (even_b, odd_b):
            weights = jnp.exp2(dot_nt(q * mask, k)).astype(BF16)
            outs.append(dot(weights, v1))
        return outs

    def attend_into(q_ref, k_ref, v_ref, rows):
        pieces = []
        for p in range(pairs):
            cols = slice(p * LANES, (p + 1) * LANES)
            first, second = pair_attend(q_ref[rows, cols], k_ref[:, cols], v_ref[:, cols])
            num = jnp.where(low, first[:, :LANES], second[:, :LANES])
            den = jnp.where(low, first[:, LANES:], second[:, LANES:])
            pieces.append((num / den).astype(BF16))
        return jnp.concatenate(pieces, axis=1)

    l_lat.wait()
    l_rq.wait()
    own_normed = rms(lat_all[mine, :])
    for t in range(tiles):
        cols = slice(t * TILE, (t + 1) * TILE)
        q = head_norm(dot(own_normed, b_rq[:, cols]), 0, t, to_exp2).astype(BF16)
        for j in range(per_tile):
            q_send[t * per_tile + j] = q[:, j * LANES : (j + 1) * LANES]
    q_all[mine, :] = q_send[my_head // 2]

    pl.semaphore_wait(barrier, n - 1)

    send_q = [
        remote(0, k, q_send.at[peers[k] // (2 * share)], q_all.at[mine], peers[k])
        for k in range(n - 1)
    ]
    for copy in send_q:
        copy.start()

    my_tokens = rows_of(me, count)
    send_kv = [
        remote(1, k, kv_send.at[peers[k] // share], kv_all.at[my_tokens], peers[k])
        for k in range(n - 1)
    ]
    l_tok.wait()
    ntok[...] = rms(tok[...])
    l_rkv.wait()
    for t in range(tiles):
        cols = slice(t * TILE, (t + 1) * TILE)
        vcols = slice(inner + t * TILE, inner + (t + 1) * TILE)
        keys = head_norm(dot(ntok[...], b_rkv[:, cols]), 1, t)
        values = dot(ntok[...], b_rkv[:, vcols])
        for j in range(per_tile):
            part = slice(j * LANES, (j + 1) * LANES)
            k, v = keys[:, part], pltpu.roll(values[:, part], width, 1)
            head = 2 * (t * per_tile + j)
            kv_send[head] = jnp.where(low, k, v).astype(BF16)
            kv_send[head + 1] = jnp.where(low, v, k).astype(BF16)
        for k in range(n - 1):
            pl.when(peers[k] // (share * 2 * per_tile) == t)(send_kv[k].start)
    kv_all[my_tokens, :] = kv_send[my_head]

    send_lat = [
        remote(2, j - 1, latents, lat_all.at[mine], lax.rem(me + 2 * j, n))
        for j in range(1, chips)
    ]
    send_lat.append(remote(2, chips - 1, latents, lat_all.at[mine], partner))
    for copy in send_lat:
        copy.start()

    l_wq.wait()
    for t in range(tiles):
        cols = slice(t * TILE, (t + 1) * TILE)
        wq[:, cols] = head_norm(dot(ntok[...], b_wq[:, cols]), 4, t, to_exp2).astype(BF16)

    for copy in send_q:
        copy.wait_recv()
    parity = lax.rem(my_head, 2)
    mine_b = jnp.where(lane // width == parity, 1.0, 0.0).astype(BF16)
    q = q_all[rows_of(lax.rem(me, share), block), :] * mine_b
    total = None
    for k in range(n):
        if k:
            send_kv[k - 1].wait_recv()
        kv = kv_all[rows_of(sources[k - 1] if k else me, count), :]
        weights = jnp.exp2(dot_nt(q, kv)).astype(BF16)
        term = dot(weights, jnp.concatenate([kv, jnp.ones_like(kv)], axis=1))
        total = term if total is None else total + term
    quotient = total[:, :LANES] / total[:, LANES:]
    message = jnp.where(
        lane // width == parity, pltpu.roll(quotient[:half], width, 1), quotient[half:]
    )
    heads_all[me] = message.astype(BF16)
    gather_att = [
        remote(3, k, heads_all.at[me], heads_all.at[me], peers[k]) for k in range(n - 1)
    ]
    for copy in gather_att:
        copy.start()

    relay_lat = []
    for j in range(1, chips):
        send_lat[j - 1].wait_recv()
        theirs = rows_of(lax.rem(me + n - 2 * j, n), own)
        copy = remote(2, chips - 1 + j, lat_all.at[theirs], lat_all.at[theirs], partner)
        copy.start()
        relay_lat.append(copy)
    send_lat[chips - 1].wait_recv()
    for copy in relay_lat:
        copy.wait_recv()

    l_ro.wait()
    l_sqkv.wait()
    for copy in gather_att:
        copy.wait_recv()
    for p in range(pairs):
        cols = slice(p * LANES, (p + 1) * LANES)
        for b in range(share):
            first = heads_all[2 * p * share + b].astype(F32)
            second = heads_all[(2 * p + 1) * share + b].astype(F32)
            top = jnp.where(low, first, second)
            bottom = pltpu.roll(jnp.where(low, second, first), width, 1)
            att[b * block : b * block + half, cols] = top.astype(BF16)
            att[b * block + half : (b + 1) * block, cols] = bottom.astype(BF16)

    def self_project(rows):
        new = lat_all[rows, :].astype(F32) + dot(att[rows, :], b_ro[...])
        new = new.astype(BF16)
        rlat[rows, :] = new
        normed[rows, :] = rms(new)
        for t in range(tiles):
            cols = slice(t * TILE, (t + 1) * TILE)
            for which, (ref, index, scale) in enumerate(
                ((sq, 2, to_exp2), (sk, 3, None), (sv, None, None))
            ):
                start = which * inner + t * TILE
                y = dot(normed[rows, :], b_sqkv[:, start : start + TILE])
                y = y if index is None else head_norm(y, index, t, scale)
                ref[rows, cols] = y.astype(BF16)

    row_blocks(every, self_project)

    l_so.wait()
    l_wkv.wait()

    def self_attend(rows):
        attended = attend_into(sq, sk, sv, rows)
        new = rlat[rows, :].astype(F32) + dot(attended, b_so[...])
        new = new.astype(BF16)
        rlat[rows, :] = new
        normed[rows, :] = rms(new)
        for t in range(tiles):
            cols = slice(t * TILE, (t + 1) * TILE)
            wk[rows, cols] = head_norm(dot(normed[rows, :], b_wkv[:, cols]), 5, t).astype(BF16)
            vcols = slice(inner + t * TILE, inner + (t + 1) * TILE)
            wv[rows, cols] = dot(normed[rows, :], b_wkv[:, vcols]).astype(BF16)

    row_blocks(every, self_attend)
    lat_out[...] = rlat[mine, :]

    l_wo.wait()
    attended = attend_into(wq, wk, wv, slice(None))
    tok_out[...] = (tok[...].astype(F32) + dot(attended, b_wo[...])).astype(BF16)

    for copy in send_q + send_kv + send_lat + relay_lat + gather_att:
        copy.wait_send()


def per_device(n, tokens, latents, *weights_and_gain):
    weights, gain = weights_and_gain[:-1], weights_and_gain[-1]
    own, d = latents.shape
    count = tokens.shape[0]
    inner = weights[0].shape[1]
    every = n * own
    hbm = pl.BlockSpec(memory_space=pl.ANY)
    vmem = pl.BlockSpec(memory_space=pltpu.VMEM)

    def buf(*shape):
        return pltpu.VMEM(shape, BF16)

    return pl.pallas_call(
        functools.partial(kernel, n),
        out_shape=(
            pltpu.VMEM(tokens.shape, BF16),
            pltpu.VMEM(latents.shape, BF16),
        ),
        in_specs=[hbm] * 10 + [vmem],
        out_specs=(vmem, vmem),
        scratch_shapes=[
            buf(count, d),
            buf(every, d),
            *[buf(*w.shape) for w in weights],
            buf(count, d),
            buf(count, inner),
            buf(inner // LANES, own, LANES),
            buf(every, LANES),
            buf(HEADS, count, LANES),
            buf(n * count, LANES),
            buf(n, every * HEADS // n // 2, LANES),
            buf(every, inner),
            buf(every, d),
            buf(every, d),
            *[buf(every, inner) for _ in range(5)],
            buf(TILE, TILE),
            pltpu.SemaphoreType.DMA((10,)),
            pltpu.SemaphoreType.DMA((4, n - 1)),
            pltpu.SemaphoreType.DMA((4, n - 1)),
        ],
        compiler_params=pltpu.CompilerParams(
            collective_id=0, has_side_effects=True, vmem_limit_bytes=67043328 - 1000 * 1024
        ),
        name="rin_block",
    )(tokens, latents, *weights, gain)


def solution(mesh):
    rows = P(("ba", "aa"), None)
    return jax.shard_map(
        functools.partial(per_device, mesh.shape["aa"]),
        mesh=mesh,
        in_specs=(rows, rows) + (P(),) * 9,
        out_specs=(rows, rows),
        check_vma=False,
    )
```
